32 devices in a mesh: grp: 1, row: 8 (over z, y), col: 4 (over x, core).
Axes of the slice: x: 2, y: 2, z: 4, core: 2. Of those that a mesh axis runs over, the one named last changes fastest.
Arguments:
- pair_act: bfloat16 [128, 128, 128], P(('grp', 'row'), 'col'), may hold values from -6 to 6
- single: bfloat16 [128, 768], P(('grp', 'row')), may hold values from -6 to 6
- token_mask: int32 [128], P('grp'), may hold values from 0 to 1, as said below
- chain_index: int32 [128], P('grp'), may hold values from 0 to 7, never falling along the last dimension, each value on 1 to 32 neighbouring positions
- residue_index: int32 [128], P('grp'), may hold values from 1 to 192, as said below
- tri_gain: float32 [2, 128], replicated, may hold values from 0.25 to 1.75
- tri_qk: bfloat16 [2, 128, 256], replicated, may hold values from -1.5 to 1.5
- tri_vg: bfloat16 [2, 128, 256], replicated, may hold values from -0.5 to 0.5
- tri_out: bfloat16 [2, 128, 128], replicated, may hold values from -0.5 to 0.5
- bias_gain: float32 [128], replicated, may hold values from 0.25 to 1.75
- bias_proj: bfloat16 [128, 16], replicated, may hold values from -0.5 to 0.5
- chain_bias: float32 [16], P('col'), may hold values from -4 to 4
- pos_slope: float32 [16], P('col'), may hold values from -6 to 6
- attn_gain: float32 [768], replicated, may hold values from 0.25 to 1.75
- attn_qk: bfloat16 [2, 768, 768], P(None, None, 'col'), may hold values from -0.375 to 0.375
- attn_vg: bfloat16 [2, 768, 768], P(None, None, 'col'), may hold values from -0.21875 to 0.21875
- attn_out: bfloat16 [768, 768], P('col'), may hold values from -0.875 to 0.875
Outputs:
- pair_out: bfloat16 [128, 128, 128], P(('grp', 'row'), 'col')
- token_update: bfloat16 [128, 768], P(('grp', 'row'), 'col')
The draws below stay inside these ranges and needn't reach their ends.
Inputs may be any that keep to these rules, and one draw needn't show every extreme that they name: `token_mask`: 1 on a leading run of at least 64 positions, 0 on the rest, and some position is 0. `chain_index`: never decreasing along the positions; all 8 chains occur. `residue_index`: starts at 1 and rises by 1 or 2 from each position to the next, by 2 at exactly 64 of them.
All inputs are finite; a program needn't handle non-finite values.
Results may differ from the reference program's by a relative error of at most 0.019.
Values may be sent and summed in bfloat16 or wider, within the bound.
No kernel may reach another device: no remote copies, remote signals or barrier semaphores. Data moves between devices by JAX's collectives and lax.ppermute only.
A program may use at most 64 MiB of HBM per device.

```python
import math
import jax
import jax.numpy as jnp
import numpy as np
from jax import lax

TOKENS = 128
C = 128
TRI_HEADS = 8
TRI_DIM = 16
D = 768
HEADS = 16
HEAD_DIM = 48
N_ROW = 8


def draw_token_mask(key, part):
    length = jax.random.randint(key, (), TOKENS // 2, TOKENS)
    return (jnp.arange(TOKENS) < length).astype(jnp.int32)


def draw_residue_index(key, part):
    order = jax.random.permutation(jax.random.fold_in(key, 7), TOKENS - 1)
    steps_drawn = jnp.where(order < TOKENS // 2, 2, 1).astype(jnp.int32)
    running_sum = jnp.concatenate([jnp.zeros((1,), jnp.int32), jnp.cumsum(steps_drawn).astype(jnp.int32)])
    return (running_sum + 1).astype(jnp.int32)


def levels(own_key, shape, cuts, smallest, high):
    level = 1.0
    for position, blocks in cuts:
        heights = jax.random.uniform(jax.random.fold_in(jax.random.fold_in(own_key, 6), position), (blocks,), jnp.float32, smallest / len(cuts), high / len(cuts))
        level = level * jnp.repeat(jnp.exp(heights), shape[position] // blocks).reshape((-1,) + (1,) * (len(shape) - 1 - position))
    return level


def length_profile(number_of, total, reach, lean):
    portions = [(1 << 20) // math.isqrt(rank ** lean) + 1 for rank in range(2, number_of + 1)]
    rest, holding = total - reach - (number_of - 1), [1] * (number_of - 1)
    while rest > 0:
        candidates = [i for i in range(number_of - 1) if holding[i] < reach]
        pool, left = sum([portions[i] for i in candidates]), rest
        for i in candidates:
            addition = min(reach - holding[i], max(1, left * portions[i] // pool), rest)
            holding[i] = holding[i] + addition
            rest = rest - addition
    return np.array([reach] + holding)


def ragged_sizes(own_key, count, total, most, skew):
    if count == 2:
        one = jax.random.randint(own_key, (), max(1, total - most), min(most, total - 1) + 1)
        return jnp.stack([one, total - one])
    lengths = jnp.asarray(length_profile(count, total, most, skew), jnp.int32)
    couples = (count - 1) // 2
    giver, sink = lengths[1:1 + 2 * couples:2], lengths[2:2 + 2 * couples:2]
    slack = jnp.minimum(giver - 1, most - sink)
    moved = jax.random.randint(jax.random.fold_in(own_key, 1), (couples,), 0, 1 << 20) % (slack + 1)
    lengths = lengths.at[1:1 + 2 * couples:2].set(giver - moved).at[2:2 + 2 * couples:2].set(sink + moved)
    return lengths[jax.random.permutation(jax.random.fold_in(own_key, 2), count)]


def gaussian(key, shape, width, reach, shards=(), kind=jnp.bfloat16):
    level = levels(key, shape, shards, -0.22, 0.18) if shards else 1.0
    entries = jax.random.normal(key, shape, jnp.float32) * width * level
    return jnp.minimum(jnp.maximum(entries, -reach), reach).astype(kind)


def setup_inputs(seed: int = 0, part: int = 0) -> dict:
    splits = jax.random.split(jax.random.key(seed), 18)
    own_keys = jax.random.split(jax.random.fold_in(splits[17], part), 18)
    pair_act = gaussian(own_keys[0], (TOKENS, TOKENS, C), 1.0, 6.0, ((0, 8), (1, 4)))
    single = gaussian(own_keys[1], (TOKENS, D), 1.0, 6.0, ((0, 8),))
    token_mask = draw_token_mask(jax.random.fold_in(jax.random.fold_in(splits[17], part), 71), part)
    chain_index = jnp.searchsorted(jnp.cumsum(ragged_sizes(own_keys[3], 8, TOKENS, TOKENS // 4, 0)), jnp.arange(TOKENS), side="right").astype(jnp.int32)
    residue_index = draw_residue_index(jax.random.fold_in(jax.random.fold_in(splits[17], part), 71), part)
    tri_gain = jnp.clip(1.0 + 0.15 * jax.random.normal(splits[5], (2, C), jnp.float32), 0.25, 1.75)
    tri_qk = gaussian(splits[6], (2, C, 2 * C), (C // 9) ** -0.5, 1.5)
    tri_vg = gaussian(splits[7], (2, C, 2 * C), C ** -0.5, 0.5)
    tri_out = gaussian(splits[8], (2, C, C), C ** -0.5, 0.5)
    bias_gain = jnp.clip(1.0 + 0.15 * jax.random.normal(splits[9], (C,), jnp.float32), 0.25, 1.75)
    bias_proj = gaussian(splits[10], (C, HEADS), C ** -0.5, 0.5)
    chain_bias = gaussian(splits[11], (HEADS,), 1.0, 4.0, ((0, 4),), jnp.float32)
    pos_slope = jnp.clip(jax.random.uniform(splits[12], (HEADS,), jnp.float32, -6.0, 6.0) * levels(splits[12], (HEADS,), ((0, 4),), -0.4, 0.0), -6.0, 6.0)
    attn_gain = jnp.clip(1.0 + 0.15 * jax.random.normal(splits[13], (D,), jnp.float32), 0.25, 1.75)
    attn_qk = gaussian(splits[14], (2, D, D), (D // 3) ** -0.5, 0.375, ((2, 4),))
    attn_vg = gaussian(splits[15], (2, D, D), D ** -0.5, 0.21875, ((2, 4),))
    attn_out = gaussian(splits[16], (D, D), (D // 16) ** -0.5, 0.875, ((0, 4),))
    return {"pair_act": pair_act, "single": single, "token_mask": token_mask, "chain_index": chain_index, "residue_index": residue_index, "tri_gain": tri_gain, "tri_qk": tri_qk, "tri_vg": tri_vg, "tri_out": tri_out, "bias_gain": bias_gain, "bias_proj": bias_proj, "chain_bias": chain_bias, "pos_slope": pos_slope, "attn_gain": attn_gain, "attn_qk": attn_qk, "attn_vg": attn_vg, "attn_out": attn_out}


epsilon = 1e-05
cap_value = 10.0
rel_reach = 32.0
highest = lax.Precision.HIGHEST

def layer_norm(inputs, norm_gain):
    inputs = inputs.astype(jnp.float32)
    centered = inputs - lax.optimization_barrier(jnp.mean(inputs, -1, keepdims=True))
    spread = lax.optimization_barrier(jnp.mean(centered * centered, -1, keepdims=True))
    return centered * lax.rsqrt(spread + epsilon) * norm_gain

def feature(inputs):
    return jnp.where(inputs > 0, inputs + 1.0, jnp.exp(jnp.minimum(inputs, 0.0)))

def rounded(inputs):
    return lax.optimization_barrier(inputs.astype(jnp.bfloat16)).astype(jnp.float32)

def split_heads(inputs):
    return inputs.reshape(inputs.shape[:-1] + (TRI_HEADS, TRI_DIM))

def reference(pair_act, single, token_mask, chain_index, residue_index, tri_gain, tri_qk, tri_vg, tri_out, bias_gain, bias_proj, chain_bias, pos_slope, attn_gain, attn_qk, attn_vg, attn_out):
    block_rows = TOKENS // N_ROW
    mask_float = token_mask.astype(jnp.float32)
    tri_scale = 1.0 / (2.0 * TRI_DIM * math.sqrt(TOKENS))

    def row_pass(row_block):
        normed = layer_norm(row_block, tri_gain[0]).astype(jnp.bfloat16)
        query_key = jnp.dot(normed, tri_qk[0], preferred_element_type=jnp.float32)
        value_gate = jnp.dot(normed, tri_vg[0], preferred_element_type=jnp.float32)
        query_feat = feature(split_heads(query_key[..., :C]))
        key_feat = feature(split_heads(query_key[..., C:])) * mask_float[None, :, None, None]
        values = split_heads(value_gate[..., :C])
        states = jnp.einsum('ijhe,ijhf->ihef', key_feat, values, precision=highest)
        mixed_heads = tri_scale * jnp.einsum('ijhe,ihef->ijhf', query_feat, states, precision=highest)
        gate_part = value_gate[..., C:]
        update = (jax.nn.sigmoid(gate_part) * mixed_heads.reshape(gate_part.shape)).astype(jnp.bfloat16)
        return (row_block.astype(jnp.float32) + jnp.dot(update, tri_out[0], preferred_element_type=jnp.float32)).astype(jnp.bfloat16)
    pair_first = lax.map(row_pass, pair_act.reshape(N_ROW, block_rows, TOKENS, C))
    row_masks = mask_float.reshape(N_ROW, block_rows)

    def col_states(states, inputs):
        row_block, row_mask = inputs
        normed = layer_norm(row_block, tri_gain[1]).astype(jnp.bfloat16)
        key_feat = feature(split_heads(jnp.dot(normed, tri_qk[1][:, C:], preferred_element_type=jnp.float32)))
        key_feat = key_feat * row_mask[:, None, None, None]
        values = split_heads(jnp.dot(normed, tri_vg[1][:, :C], preferred_element_type=jnp.float32))
        return (states + jnp.einsum('ijhe,ijhf->jhef', key_feat, values, precision=highest), None)
    zero_states = jnp.zeros((TOKENS, TRI_HEADS, TRI_DIM, TRI_DIM), jnp.float32)
    states, unused = lax.scan(col_states, zero_states, (pair_first, row_masks))

    def col_pass(row_block):
        normed = layer_norm(row_block, tri_gain[1]).astype(jnp.bfloat16)
        query_feat = feature(split_heads(jnp.dot(normed, tri_qk[1][:, :C], preferred_element_type=jnp.float32)))
        gate_part = jnp.dot(normed, tri_vg[1][:, C:], preferred_element_type=jnp.float32)
        mixed_heads = tri_scale * jnp.einsum('ijhe,jhef->ijhf', query_feat, states, precision=highest)
        update = (jax.nn.sigmoid(gate_part) * mixed_heads.reshape(gate_part.shape)).astype(jnp.bfloat16)
        return (row_block.astype(jnp.float32) + jnp.dot(update, tri_out[1], preferred_element_type=jnp.float32)).astype(jnp.bfloat16)
    pair_second = lax.map(col_pass, pair_first)
    tok_normed = layer_norm(single, attn_gain).astype(jnp.bfloat16)
    query_all = rounded(jnp.dot(tok_normed, attn_qk[0], preferred_element_type=jnp.float32)).reshape(TOKENS, HEADS, HEAD_DIM)
    key_heads = rounded(jnp.dot(tok_normed, attn_qk[1], preferred_element_type=jnp.float32)).reshape(TOKENS, HEADS, HEAD_DIM)
    value_heads = rounded(jnp.dot(tok_normed, attn_vg[0], preferred_element_type=jnp.float32)).reshape(TOKENS, HEADS, HEAD_DIM)
    gate_all = jnp.dot(tok_normed, attn_vg[1], preferred_element_type=jnp.float32)

    def diffuse(inputs):
        pair_rows, query_rows, gate_rows, chain_rows, residue_rows = inputs
        normed = layer_norm(pair_rows, bias_gain).astype(jnp.bfloat16)
        pair_bias = rounded(jnp.dot(normed, bias_proj, preferred_element_type=jnp.float32))
        scores = jnp.einsum('ihd,jhd->hij', query_rows, key_heads, precision=highest) / math.sqrt(HEAD_DIM)
        scores = scores + jnp.transpose(pair_bias, (2, 0, 1))
        same_chain = chain_rows[:, None] == chain_index[None, :]
        offset = jnp.clip((residue_rows[:, None] - residue_index[None, :]).astype(jnp.float32), -rel_reach, rel_reach) / rel_reach
        scores = scores + jnp.where(same_chain[None], chain_bias[:, None, None] + pos_slope[:, None, None] * offset[None], 0.0)
        weights = jnp.exp(cap_value * jnp.tanh(scores / cap_value)) * mask_float[None, None, :]
        numerator = jnp.einsum('hij,jhd->ihd', rounded(weights), value_heads, precision=highest)
        denominator = lax.optimization_barrier(jnp.sum(weights, axis=2))
        attended = numerator / jnp.transpose(denominator)[:, :, None]
        gated = (jax.nn.sigmoid(gate_rows) * attended.reshape(gate_rows.shape)).astype(jnp.bfloat16)
        return jnp.dot(gated, attn_out, preferred_element_type=jnp.float32).astype(jnp.bfloat16)
    token_update = lax.map(diffuse, (pair_second, query_all.reshape(N_ROW, block_rows, HEADS, HEAD_DIM), gate_all.reshape(N_ROW, block_rows, D), chain_index.reshape(N_ROW, block_rows), residue_index.reshape(N_ROW, block_rows)))
    return (pair_second.reshape(TOKENS, TOKENS, C), token_update.reshape(TOKENS, D))
```

```python
import functools
import math

import jax
import jax.numpy as jnp
from jax import lax
from jax.experimental import pallas as pl
from jax.experimental.pallas import tpu as pltpu
from jax.sharding import PartitionSpec as P

C = 128
TRI_HEADS = 8
TRI_DIM = 16
HEAD_DIM = 48
PAD_ROWS = 8

epsilon = 1e-05
cap_value = 10.0
rel_reach = 32.0

F32 = jnp.float32
BF16 = jnp.bfloat16
VMEM = pl.BlockSpec(memory_space=pltpu.VMEM)
SMEM = pl.BlockSpec(memory_space=pltpu.SMEM)


def mm(a, b):
    return jnp.dot(a, b, preferred_element_type=F32)


def mm_nt(a, b):
    return lax.dot_general(a, b, (((1,), (1,)), ((), ())), preferred_element_type=F32)


def mm_tn(a, b):
    return lax.dot_general(a, b, (((0,), (0,)), ((), ())), preferred_element_type=F32)


def iota(shape, dim):
    return lax.broadcasted_iota(jnp.int32, shape, dim)


def layer_norm(x, gain):
    centered = x - jnp.mean(x, -1, keepdims=True)
    spread = jnp.mean(centered * centered, -1, keepdims=True)
    return centered * lax.rsqrt(spread + epsilon) * gain


def feature(x):
    return jnp.where(x > 0, x + 1.0, jnp.exp(jnp.minimum(x, 0.0)))


def sigmoid(x):
    return 1.0 / (1.0 + jnp.exp(-x))


def triangle(x, lines, length, gain, qk, vg, out, scale):
    tokens = x.shape[0] // lines
    normed = layer_norm(x, gain).astype(BF16)
    query_key = mm(normed, qk)
    value_gate = mm(normed, vg)
    valid = iota((tokens, C), 0) < length
    same_head = (iota((C, C), 0) // TRI_DIM) == (iota((C, C), 1) // TRI_DIM)
    lines_out = []
    for line in range(lines):
        rows = slice(line * tokens, (line + 1) * tokens)
        query = feature(query_key[rows, :C]).astype(BF16)
        key = jnp.where(valid, feature(query_key[rows, C:]), 0.0).astype(BF16)
        values = value_gate[rows, :C].astype(BF16)
        state = jnp.where(same_head, mm_tn(key, values) * scale, 0.0).astype(BF16)
        update = (sigmoid(value_gate[rows, C:]) * mm(query, state)).astype(BF16)
        lines_out.append(x[rows] + mm(update, out))
    return lines_out


def row_kernel(scale, n_col, lines, me_ref, mask_ref, gain_ref, qk_ref, vg_ref, out_w_ref, *refs):
    pieces, z_ref, x_scr, z_scr = refs[:n_col], refs[n_col], refs[n_col + 1], refs[n_col + 2]
    block = pieces[0].shape[0] // lines
    tokens = block * n_col
    me = me_ref[0]
    for k in range(n_col):
        source = me ^ k
        for line in range(lines):
            start = pl.multiple_of(line * tokens + source * block, block)
            x_scr[pl.ds(start, block), :] = pieces[k][line * block : (line + 1) * block, :].astype(F32)
    length = jnp.sum(mask_ref[...])
    done = triangle(
        x_scr[...], lines, length, gain_ref[0:1, :], qk_ref[0], vg_ref[0], out_w_ref[0], scale
    )
    for line in range(lines):
        z_scr[line * tokens : (line + 1) * tokens, :] = done[line]
    owners, per_owner, _ = z_ref.shape
    for d in range(owners):
        z_ref[d] = z_scr[pl.ds(d, per_owner, stride=owners), :].astype(BF16)


def col_kernel(
    scale, n_row, n_col, row_count, col_count, heads_here,
    mask_ref, gain_ref, qk_ref, vg_ref, out_w_ref, bias_gain_ref, bias_proj_ref, z_ref, out_ref, z_scr,
):
    lines = z_scr.shape[0] // (n_row * row_count)
    tokens = n_row * row_count
    devices = n_row * n_col
    z_scr[...] = z_ref[...].astype(F32)
    x = jnp.concatenate([z_scr[pl.ds(line, tokens, stride=lines), :] for line in range(lines)], axis=0)
    length = jnp.sum(mask_ref[...])
    done = triangle(x, lines, length, gain_ref[1:2, :], qk_ref[1], vg_ref[1], out_w_ref[1], scale)
    done = [part.astype(BF16) for part in done]
    normed = [layer_norm(part.astype(F32), bias_gain_ref[...]).astype(BF16) for part in done]
    width = lines * row_count
    for r in range(n_row):
        rows = slice(r * row_count, (r + 1) * row_count)
        bias = mm_nt(bias_proj_ref[...], jnp.concatenate([part[rows] for part in normed], axis=0))
        for c in range(n_col):
            dest = r * n_col + c
            out_ref[dest, :row_count, :] = done[c * col_count // devices][rows]
            out_ref[dest, row_count:, :] = jnp.zeros((PAD_ROWS, C), BF16)
            out_ref[dest, row_count : row_count + heads_here, :width] = bias[
                c * heads_here : (c + 1) * heads_here, :
            ].astype(BF16)


def token_kernel(single_ref, gain_ref, qk_ref, vg_ref, q_ref, kv_ref, g_ref):
    width = q_ref.shape[1]
    normed = layer_norm(single_ref[...].astype(F32), gain_ref[...]).astype(BF16)
    q_ref[...] = mm_nt(normed, qk_ref[0]).astype(BF16)
    kv_ref[0] = mm_nt(normed, qk_ref[1]).astype(BF16)
    kv_ref[1] = mm_nt(normed, vg_ref[0]).astype(BF16)
    g_ref[...] = mm_nt(normed, vg_ref[1])


def attn_kernel(
    n_row, n_col, row_count, heads_here,
    me_ref, chain_bias_ref, slope_ref, mask_ref, chain_ref, residue_ref, q_ref, g_ref, out_w_ref, got_ref, *refs,
):
    kv_refs, o_ref, k_scr, v_scr = refs[:-3], refs[-3], refs[-2], refs[-1]
    tokens = n_row * row_count
    devices = n_row * n_col
    lines = tokens // devices
    width = heads_here * HEAD_DIM
    me = me_ref[0]
    slot = 0
    for ref in kv_refs:
        for t in range(ref.shape[0]):
            start = pl.multiple_of((me ^ slot) * row_count, row_count)
            k_scr[pl.ds(start, row_count), :] = ref[t, 0].astype(F32)
            v_scr[pl.ds(start, row_count), :] = ref[t, 1].astype(F32)
            slot += 1
    keys, values = k_scr[...].astype(BF16), v_scr[...].astype(BF16)

    own = iota((row_count, tokens), 1) == iota((row_count, tokens), 0) + me * row_count
    chain = chain_ref[...].astype(F32)
    residue = residue_ref[...].astype(F32)
    my_chain = jnp.sum(jnp.where(own, chain, 0.0), -1, keepdims=True)
    my_residue = jnp.sum(jnp.where(own, residue, 0.0), -1, keepdims=True)
    same_chain = my_chain == chain
    offset = jnp.clip(my_residue - residue, -rel_reach, rel_reach) / rel_reach
    length = jnp.sum(mask_ref[...])
    valid = iota((row_count, tokens), 1) < length

    count = devices * PAD_ROWS
    got = got_ref[:, row_count:, :].astype(F32).reshape(count, C).astype(BF16)
    src, dst = iota((count, heads_here * devices), 0), iota((count, heads_here * devices), 1)
    place = ((src % PAD_ROWS == dst // devices) & (src // PAD_ROWS == dst % devices)).astype(F32).astype(BF16)
    turned = mm_tn(got, place)

    head_of = iota((row_count, width), 1) // HEAD_DIM
    query = q_ref[...].astype(F32)
    stacked = jnp.concatenate(
        [jnp.where(head_of == h, query, 0.0) for h in range(heads_here)], axis=0
    ).astype(BF16)
    scores = mm_nt(stacked, keys) / math.sqrt(HEAD_DIM)
    weights = []
    for h in range(heads_here):
        bias = jnp.concatenate(
            [
                turned[line * row_count : (line + 1) * row_count, h * devices : (h + 1) * devices]
                for line in range(lines)
            ],
            axis=1,
        )
        e = scores[h * row_count : (h + 1) * row_count] + bias
        e = e + jnp.where(same_chain, chain_bias_ref[h] + slope_ref[h] * offset, 0.0)
        weights.append(jnp.where(valid, jnp.exp(cap_value * jnp.tanh(e / cap_value)), 0.0))
    numerator = mm(jnp.concatenate(weights, axis=0).astype(BF16), values)
    attended = jnp.zeros((row_count, width), F32)
    for h in range(heads_here):
        part = numerator[h * row_count : (h + 1) * row_count] / jnp.sum(weights[h], -1, keepdims=True)
        attended = jnp.where(head_of == h, part, attended)
    gated = (sigmoid(g_ref[...]) * attended).astype(BF16)
    full = mm(gated, out_w_ref[...])
    share = full.shape[1] // n_col
    for c in range(n_col):
        o_ref[c] = full[:, c * share : (c + 1) * share].astype(BF16)


def pair_kernel(row_count, got_ref, out_ref, scr):
    sources = got_ref.shape[0]
    scr[...] = got_ref[:, :row_count, :].astype(F32).reshape(sources * row_count, C)
    for i in range(row_count):
        out_ref[i] = scr[pl.ds(i, sources, stride=row_count), :].astype(BF16)


def swap_col(blocks, me, n_col):
    pieces = []
    for k in range(n_col):
        piece = lax.dynamic_index_in_dim(blocks, me ^ k, 0, keepdims=False)
        if k:
            piece = lax.ppermute(piece, "col", [(i, i ^ k) for i in range(n_col)])
        pieces.append(piece)
    return pieces


def on_device(
    n_row, n_col,
    pair_act, single, token_mask, chain_index, residue_index, tri_gain, tri_qk, tri_vg, tri_out,
    bias_gain, bias_proj, chain_bias, pos_slope, attn_gain, attn_qk, attn_vg, attn_out,
):
    tokens = token_mask.shape[0]
    row_count, col_count = pair_act.shape[0], pair_act.shape[1]
    heads_here = chain_bias.shape[0]
    devices = n_row * n_col
    own_rows, own_cols = row_count // n_col, tokens // devices
    scale = 1.0 / (2.0 * TRI_DIM * math.sqrt(tokens))
    my_row, my_col = lax.axis_index("row"), lax.axis_index("col")
    row_id, col_id = my_row.reshape(1), my_col.reshape(1)
    mask2 = token_mask.reshape(1, tokens)
    width = heads_here * HEAD_DIM

    pieces = swap_col(pair_act.reshape(n_col, own_rows * col_count, C), my_col, n_col)
    per_owner = own_rows * own_cols
    z_out = pl.pallas_call(
        functools.partial(row_kernel, scale, n_col, own_rows),
        out_shape=jax.ShapeDtypeStruct((devices, per_owner, C), BF16),
        in_specs=[SMEM] + [VMEM] * (5 + n_col),
        out_specs=VMEM,
        scratch_shapes=[pltpu.VMEM((own_rows * tokens, C), F32)] * 2,
        name="row_pass",
    )(col_id, mask2, tri_gain, tri_qk, tri_vg, tri_out, *pieces)

    z_in = lax.all_to_all(z_out, ("row", "col"), 0, 0, tiled=True)
    back = pl.pallas_call(
        functools.partial(col_kernel, scale, n_row, n_col, row_count, col_count, heads_here),
        out_shape=jax.ShapeDtypeStruct((devices, row_count + PAD_ROWS, C), BF16),
        in_specs=[VMEM] * 8,
        out_specs=VMEM,
        scratch_shapes=[pltpu.VMEM((own_cols * tokens, C), F32)],
        name="col_pass",
    )(
        mask2, tri_gain, tri_qk, tri_vg, tri_out, bias_gain.reshape(1, C), bias_proj.T,
        z_in.reshape(own_cols * tokens, C),
    )
    got = lax.all_to_all(back, ("row", "col"), 0, 0, tiled=True)

    query, kv, gate = pl.pallas_call(
        token_kernel,
        out_shape=(
            jax.ShapeDtypeStruct((row_count, width), BF16),
            jax.ShapeDtypeStruct((2, row_count, width), BF16),
            jax.ShapeDtypeStruct((row_count, width), F32),
        ),
        in_specs=[VMEM] * 4,
        out_specs=(VMEM,) * 3,
        name="token_proj",
    )(single, attn_gain.reshape(1, -1), attn_qk.swapaxes(1, 2), attn_vg.swapaxes(1, 2))
    held = [kv[None]]
    step = 1
    while step < n_row:
        sent = held[0] if len(held) == 1 else jnp.concatenate(held, axis=0)
        held.append(lax.ppermute(sent, "row", [(i, i ^ step) for i in range(n_row)]))
        step *= 2

    terms = pl.pallas_call(
        functools.partial(attn_kernel, n_row, n_col, row_count, heads_here),
        out_shape=jax.ShapeDtypeStruct((n_col, row_count, attn_out.shape[1] // n_col), BF16),
        in_specs=[SMEM] * 3 + [VMEM] * (7 + len(held)),
        out_specs=VMEM,
        scratch_shapes=[pltpu.VMEM((tokens, width), F32)] * 2,
        name="token_attention",
    )(
        row_id, chain_bias, pos_slope, mask2, chain_index.reshape(1, tokens), residue_index.reshape(1, tokens),
        query, gate, attn_out, got, *held,
    )
    parts = swap_col(terms, my_col, n_col)
    token_update = sum(part.astype(F32) for part in parts).astype(BF16)

    first = my_col * col_count % devices
    mine = got if col_count == devices else lax.dynamic_slice_in_dim(got, first, col_count, 0)
    pair_out = pl.pallas_call(
        functools.partial(pair_kernel, row_count),
        out_shape=jax.ShapeDtypeStruct((row_count, col_count, C), BF16),
        in_specs=[VMEM],
        out_specs=VMEM,
        scratch_shapes=[pltpu.VMEM((col_count * row_count, C), F32)],
        name="pair_order",
    )(mine)
    return (pair_out, token_update)


def solution(mesh):
    return jax.shard_map(
        functools.partial(on_device, mesh.shape["row"], mesh.shape["col"]),
        mesh=mesh,
        in_specs=(
            P(("grp", "row"), "col", None),
            P(("grp", "row"), None),
            P("grp"),
            P("grp"),
            P("grp"),
            P(),
            P(),
            P(),
            P(),
            P(),
            P(),
            P("col"),
            P("col"),
            P(),
            P(None, None, "col"),
            P(None, None, "col"),
            P("col", None),
        ),
        out_specs=(P(("grp", "row"), "col", None), P(("grp", "row"), "col")),
        check_vma=False,
    )
```

```python
import functools
import math

import jax
import jax.numpy as jnp
from jax import lax
from jax.experimental import pallas as pl
from jax.experimental.pallas import tpu as pltpu
from jax.sharding import PartitionSpec as P


C = 128
TRI_DIM = 16
HEAD_DIM = 48
LANES = 128

epsilon = 1e-05
cap_value = 10.0
rel_reach = 32.0

F32 = jnp.float32
BF16 = jnp.bfloat16
VMEM = pl.BlockSpec(memory_space=pltpu.VMEM)
SMEM = pl.BlockSpec(memory_space=pltpu.SMEM)
ANY = pl.BlockSpec(memory_space=pl.ANY)


def on_chip(x):
    return pltpu.with_memory_space_constraint(x, pltpu.VMEM)


def call(kernel, out_shape, smem, near=(), far=(), scratch=()):
    many = isinstance(out_shape, (tuple, list))
    return pl.pallas_call(
        kernel,
        out_shape=out_shape,
        in_specs=[SMEM] * len(smem) + [VMEM] * len(near) + [ANY] * len(far),
        out_specs=tuple([VMEM] * len(out_shape)) if many else VMEM,
        scratch_shapes=list(scratch),
    )(*smem, *[on_chip(x) for x in near], *far)


def chip(x):
    return pltpu.VMEM(x.shape, x.dtype)


def mm(a, b):
    return jnp.dot(a, b, preferred_element_type=F32)


def mm_nt(a, b):
    return lax.dot_general(a, b, (((1,), (1,)), ((), ())), preferred_element_type=F32)


def mm_tn(a, b):
    return lax.dot_general(a, b, (((0,), (0,)), ((), ())), preferred_element_type=F32)


def iota(shape, dim):
    return lax.broadcasted_iota(jnp.int32, shape, dim)


def layer_norm(x, gain):
    centered = x - jnp.mean(x, -1, keepdims=True)
    spread = jnp.mean(centered * centered, -1, keepdims=True)
    return centered * lax.rsqrt(spread + epsilon) * gain


def feature(x):
    return jnp.where(x > 0, x + 1.0, jnp.exp(jnp.minimum(x, 0.0)))


def sigmoid(x):
    return 1.0 / (1.0 + jnp.exp(-x))


def triangle(x, lines, length, gain, qk, vg, out, scale):
    tokens = x.shape[0] // lines
    normed = layer_norm(x, gain).astype(BF16)
    query_key = mm(normed, qk)
    value_gate = mm(normed, vg)
    valid = iota((tokens, C), 0) < length
    same_head = (iota((C, C), 0) // TRI_DIM) == (iota((C, C), 1) // TRI_DIM)
    lines_out = []
    for line in range(lines):
        rows = slice(line * tokens, (line + 1) * tokens)
        query = feature(query_key[rows, :C]).astype(BF16)
        key = jnp.where(valid, feature(query_key[rows, C:]), 0.0).astype(BF16)
        values = value_gate[rows, :C].astype(BF16)
        state = jnp.where(same_head, mm_tn(key, values) * scale, 0.0).astype(BF16)
        update = (sigmoid(value_gate[rows, C:]) * mm(query, state)).astype(BF16)
        lines_out.append(x[rows] + mm(update, out))
    return lines_out


def row_kernel(scale, n_col, lines, mask_ref, gain_ref, qk_ref, vg_ref, out_w_ref, own_ref, *refs):
    pieces, z_ref, x_scr, z_scr = refs[:-3], refs[-3], refs[-2], refs[-1]
    block = own_ref.shape[0] // lines
    tokens = block * n_col
    me = lax.axis_index("col")
    for k in range(n_col):
        source = me ^ k
        for line in range(lines):
            start = pl.multiple_of(line * tokens + source * block, block)
            rows = slice(line * block, (line + 1) * block)
            piece = pieces[k - 1][rows, :] if k else own_ref[rows, :]
            x_scr[pl.ds(start, block), :] = piece.astype(F32)
    length = jnp.sum(mask_ref[...])
    done = triangle(
        x_scr[...], lines, length, gain_ref[0:1, :], qk_ref[0], vg_ref[0], out_w_ref[0], scale
    )
    for line in range(lines):
        z_scr[line * tokens : (line + 1) * tokens, :] = done[line]
    owners, per_owner, _ = z_ref.shape
    for d in range(owners):
        z_ref[d] = z_scr[pl.ds(d, per_owner, stride=owners), :].astype(BF16)


def bias_form(row_count, lines, heads_here):
    side = LANES // (row_count * lines)
    return side, heads_here // side


def col_kernel(
    scale, n_row, n_col, row_count, col_count, heads_here,
    mask_ref, gain_ref, qk_ref, vg_ref, out_w_ref, bias_gain_ref, bias_proj_ref, z_ref, out_ref, z_scr, out_scr,
):
    lines = z_scr.shape[0] // (n_row * row_count)
    tokens = n_row * row_count
    devices = n_row * n_col
    z_scr[...] = z_ref[...].astype(F32)
    x = jnp.concatenate([z_scr[pl.ds(line, tokens, stride=lines), :] for line in range(lines)], axis=0)
    length = jnp.sum(mask_ref[...])
    done = triangle(x, lines, length, gain_ref[1:2, :], qk_ref[1], vg_ref[1], out_w_ref[1], scale)
    done = [part.astype(BF16).astype(F32) for part in done]
    normed = [layer_norm(part, bias_gain_ref[...]).astype(BF16) for part in done]
    side, deep = bias_form(row_count, lines, heads_here)
    chunk = row_count + deep
    proj = bias_proj_ref[...].astype(F32)
    projs = []
    for g in range(side):
        first = [c * heads_here + g * deep for c in range(n_col)]
        projs.append(jnp.concatenate([proj[f : f + deep] for f in first], axis=0).astype(BF16))
    for r in range(n_row):
        rows = slice(r * row_count, (r + 1) * row_count)
        here = jnp.concatenate([part[rows] for part in normed], axis=0)
        bias = jnp.concatenate([mm_nt(p, here) for p in projs], axis=1)
        for c in range(n_col):
            base = (r * n_col + c) * chunk
            out_scr[base : base + row_count, :] = done[c * col_count // devices][rows]
            out_scr[base + row_count : base + chunk, :] = bias[c * deep : (c + 1) * deep, :]
    out_ref[...] = out_scr[...].astype(BF16)


def start_all(pairs, sems):
    copies = [pltpu.make_async_copy(a, b, sems.at[n]) for n, (a, b) in enumerate(pairs)]
    for copy in copies:
        copy.start()
    return copies


def wait_all(copies):
    for copy in copies:
        copy.wait()


def kv_kernel(count, single_ref, gain_ref, wk_ref, wv_ref, x_ref, *refs):
    rest, (kv_ref, normed_ref, own_ref), rest_out, sems = (
        refs[:count], refs[count : count + 3], refs[count + 3 : -1], refs[-1],
    )
    copies = start_all([(x_ref.at[lax.axis_index("col")], own_ref), *zip(rest, rest_out)], sems)
    gain = gain_ref[...]
    gains = jnp.concatenate([gain[c : c + 1, :] for c in range(gain.shape[0])], axis=1)
    normed = layer_norm(single_ref[...].astype(F32), gains).astype(BF16)
    normed_ref[...] = normed
    kv_ref[0] = mm_nt(normed, wk_ref[...]).astype(BF16)
    kv_ref[1] = mm_nt(normed, wv_ref[...]).astype(BF16)
    wait_all(copies)


def qg_kernel(count, normed_ref, qk_ref, vg_ref, *refs):
    rest, (q_ref, g_ref), rest_out, (wq, wg, sems) = (
        refs[:count], refs[count : count + 2], refs[count + 2 : -3], refs[-3:],
    )
    copies = start_all([(qk_ref.at[0], wq), (vg_ref.at[1], wg), *zip(rest, rest_out)], sems)
    copies[0].wait()
    q_ref[...] = mm_nt(normed_ref[...], wq[...]).astype(BF16)
    copies[1].wait()
    g_ref[...] = mm_nt(normed_ref[...], wg[...])
    wait_all(copies[2:])


def attn_kernel(
    n_row, n_col, row_count, heads_here,
    slots, chain_bias_ref, slope_ref, mask_ref, chain_ref, residue_ref, q_ref, g_ref, out_w_ref, got_ref, *refs,
):
    kv_refs, o_refs, (k_scr, v_scr, o_scr, got_scr) = refs[: -4 - n_col], refs[-4 - n_col : -4], refs[-4:]
    tokens = n_row * row_count
    devices = n_row * n_col
    lines = tokens // devices
    width = heads_here * HEAD_DIM
    me = lax.axis_index("row")
    held = [(ref, t) for ref in kv_refs for t in range(ref.shape[0])]
    for slot, (ref, t) in zip(slots, held):
        start = pl.multiple_of((me ^ slot) * row_count, row_count)
        k_scr[pl.ds(start, row_count), :] = ref[t, 0].astype(F32)
        v_scr[pl.ds(start, row_count), :] = ref[t, 1].astype(F32)
    keys, values = k_scr[...].astype(BF16), v_scr[...].astype(BF16)

    own = iota((row_count, tokens), 1) == iota((row_count, tokens), 0) + me * row_count
    chain = chain_ref[...].astype(F32)
    residue = residue_ref[...].astype(F32)
    my_chain = jnp.sum(jnp.where(own, chain, 0.0), -1, keepdims=True)
    my_residue = jnp.sum(jnp.where(own, residue, 0.0), -1, keepdims=True)
    same_chain = my_chain == chain
    offset = jnp.clip(my_residue - residue, -rel_reach, rel_reach) / rel_reach
    length = jnp.sum(mask_ref[...])
    valid = iota((row_count, tokens), 1) < length

    _, deep = bias_form(row_count, lines, heads_here)
    chunk = row_count + deep
    got_scr[...] = got_ref[...].astype(F32)
    same = (iota((devices, devices), 0) == iota((devices, devices), 1)).astype(F32).astype(BF16)
    turned = [
        mm_tn(got_scr[pl.ds(row_count + a, devices, stride=chunk), :].astype(BF16), same) for a in range(deep)
    ]

    head_of = iota((row_count, width), 1) // HEAD_DIM
    query = q_ref[...].astype(F32)
    stacked = jnp.concatenate(
        [jnp.where(head_of == h, query, 0.0) for h in range(heads_here)], axis=0
    ).astype(BF16)
    scores = mm_nt(stacked, keys) / math.sqrt(HEAD_DIM)
    weights = []
    for h in range(heads_here):
        bias = jnp.concatenate(
            [
                turned[h % deep][(h // deep * lines + line) * row_count :][:row_count]
                for line in range(lines)
            ],
            axis=1,
        )
        e = scores[h * row_count : (h + 1) * row_count] + bias
        e = e + jnp.where(same_chain, chain_bias_ref[0:1, h : h + 1] + slope_ref[0:1, h : h + 1] * offset, 0.0)
        weights.append(jnp.where(valid, jnp.exp(cap_value * jnp.tanh(e / cap_value)), 0.0))
    numerator = mm(jnp.concatenate(weights, axis=0).astype(BF16), values)
    attended = jnp.zeros((row_count, width), F32)
    for h in range(heads_here):
        part = numerator[h * row_count : (h + 1) * row_count] / jnp.sum(weights[h], -1, keepdims=True)
        attended = jnp.where(head_of == h, part, attended)
    gated = (sigmoid(g_ref[...]) * attended).astype(BF16)
    full = mm(gated, out_w_ref[...])
    share = full.shape[1] // n_col
    for c in range(n_col):
        o_scr[c] = full[:, c * share : (c + 1) * share]
    for k in range(n_col):
        o_refs[k][...] = o_scr[lax.axis_index("col") ^ k].astype(BF16)


def pair_kernel(row_count, chunk, got_ref, out_ref, scr):
    scr[...] = got_ref[...].astype(F32)
    for i in range(row_count):
        out_ref[i] = scr[pl.ds(i, out_ref.shape[1], stride=chunk), :].astype(BF16)


def pick_kernel(n_col, x_ref, single_ref, gain_ref, qk_ref, vg_ref, *refs):
    sent, (single_out, gain_out, wk_out, wv_out, sems) = refs[: n_col - 1], refs[n_col - 1 :]
    me = lax.axis_index("col")
    pairs = [(x_ref.at[me ^ (k + 1)], sent[k]) for k in range(n_col - 1)]
    pairs += [(qk_ref.at[1], wk_out), (vg_ref.at[0], wv_out), (single_ref, single_out), (gain_ref, gain_out)]
    wait_all(start_all(pairs, sems))


def swap_col(blocks, n_col):
    got = []
    for k, block in enumerate(blocks, 1):
        got.append(lax.ppermute(block, "col", [(i, i ^ k) for i in range(n_col)]))
    return got


def in_layer(n_row, n_col, *args):
    return on_device(n_row, n_col, *args)


def on_device(
    n_row, n_col,
    pair_act, single, token_mask, chain_index, residue_index, tri_gain, tri_qk, tri_vg, tri_out,
    bias_gain, bias_proj, chain_bias, pos_slope, attn_gain, attn_qk, attn_vg, attn_out,
):
    tokens = token_mask.shape[0]
    row_count, col_count = pair_act.shape[0], pair_act.shape[1]
    heads_here = chain_bias.shape[0]
    devices = n_row * n_col
    own_rows, own_cols = row_count // n_col, tokens // devices
    scale = 1.0 / (2.0 * TRI_DIM * math.sqrt(tokens))
    width = heads_here * HEAD_DIM
    share = attn_out.shape[1] // n_col
    chunk = row_count + bias_form(row_count, own_cols, heads_here)[1]

    blocks = pair_act.reshape(n_col, own_rows * col_count, C)
    block = pltpu.VMEM(blocks.shape[1:], BF16)
    gain2 = attn_gain.reshape(-1, C)
    wqk, wvg = attn_qk.swapaxes(1, 2), attn_vg.swapaxes(1, 2)
    weight = pltpu.VMEM(wqk.shape[1:], BF16)
    *picked, single, gain2, wk, wv = call(
        functools.partial(pick_kernel, n_col),
        [block] * (n_col - 1) + [chip(single), chip(gain2), weight, weight],
        [], [], [blocks, single, gain2, wqk, wvg], [pltpu.SemaphoreType.DMA((n_col + 3,))],
    )
    pieces = swap_col(picked, n_col)
    early = [token_mask.reshape(1, tokens), tri_gain, tri_qk, tri_vg, tri_out]
    kv, normed, own, *early = call(
        functools.partial(kv_kernel, len(early)),
        [pltpu.VMEM((2, row_count, width), BF16), chip(single), block, *map(chip, early)],
        [], [single, gain2, wk, wv], [blocks, *early], [pltpu.SemaphoreType.DMA((1 + len(early),))],
    )
    mask, tri_gain, tri_qk, tri_vg, tri_out = early
    z_out = call(
        functools.partial(row_kernel, scale, n_col, own_rows),
        pltpu.VMEM((devices, own_rows * own_cols, C), BF16),
        [], [mask, tri_gain, tri_qk, tri_vg, tri_out, own, *pieces],
        scratch=[pltpu.VMEM((own_rows * tokens, C), F32)] * 2,
    )

    z_in = lax.all_to_all(z_out, ("row", "col"), 0, 0, tiled=True)
    late = [
        bias_gain.reshape(1, C), bias_proj.T, chain_bias.reshape(1, -1), pos_slope.reshape(1, -1),
        chain_index.reshape(1, tokens), residue_index.reshape(1, tokens), attn_out,
    ]
    query, gate, *late = call(
        functools.partial(qg_kernel, len(late)),
        [pltpu.VMEM((row_count, width), BF16), pltpu.VMEM((row_count, width), F32), *map(chip, late)],
        [], [normed], [wqk, wvg, *late], [weight, weight, pltpu.SemaphoreType.DMA((2 + len(late),))],
    )
    bias_gain, bias_proj, chain_bias, pos_slope, chain, residue, attn_out = late
    back = call(
        functools.partial(col_kernel, scale, n_row, n_col, row_count, col_count, heads_here),
        pltpu.VMEM((devices * chunk, C), BF16),
        [],
        [
            mask, tri_gain, tri_qk, tri_vg, tri_out, bias_gain, bias_proj,
            z_in.reshape(own_cols * tokens, C),
        ],
        scratch=[pltpu.VMEM((own_cols * tokens, C), F32), pltpu.VMEM((devices * chunk, C), F32)],
    )
    got = lax.all_to_all(back.reshape(devices, chunk // 2, 2, C), ("row", "col"), 0, 0, tiled=True)
    got = got.reshape(devices * chunk, C)

    held, slots = [kv[None]], [0]
    for step in kv_steps(n_row):
        sent = held[0] if len(held) == 1 else jnp.concatenate(held, axis=0)
        held.append(lax.ppermute(sent, "row", [(i, i ^ step) for i in range(n_row)]))
        slots += [slot ^ step for slot in slots]

    terms = call(
        functools.partial(attn_kernel, n_row, n_col, row_count, heads_here, slots),
        [pltpu.VMEM((row_count, share), BF16)] * n_col,
        [],
        [chain_bias, pos_slope, mask, chain, residue, query, gate, attn_out, got, *held],
        scratch=[pltpu.VMEM((tokens, width), F32)] * 2
        + [pltpu.VMEM((n_col, row_count, share), F32), pltpu.VMEM((devices * chunk, C), F32)],
    )
    parts = [terms[0]] + swap_col(terms[1:], n_col)
    token_update = sum(part.astype(F32) for part in parts).astype(BF16)

    first = lax.axis_index("col") * col_count % devices
    mine = got if col_count == devices else lax.dynamic_slice_in_dim(got, first * chunk, col_count * chunk, 0)
    pair_out = call(
        functools.partial(pair_kernel, row_count, chunk),
        jax.ShapeDtypeStruct((row_count, col_count, C), BF16),
        [], [mine], scratch=[pltpu.VMEM((col_count * chunk, C), F32)],
    )
    return (pair_out, token_update)


def kv_steps(n_row):
    return [1 << b for b in range((n_row - 1).bit_length())]


def solution(mesh):
    return jax.shard_map(
        functools.partial(in_layer, mesh.shape["row"], mesh.shape["col"]),
        mesh=mesh,
        in_specs=(
            P(("grp", "row"), "col", None),
            P(("grp", "row"), None),
            P("grp"),
            P("grp"),
            P("grp"),
            P(),
            P(),
            P(),
            P(),
            P(),
            P(),
            P("col"),
            P("col"),
            P(),
            P(None, None, "col"),
            P(None, None, "col"),
            P("col", None),
        ),
        out_specs=(P(("grp", "row"), "col", None), P(("grp", "row"), "col")),
        check_vma=False,
    )
```

```python
import functools
import math

import jax
import jax.numpy as jnp
from jax import lax
from jax.experimental import pallas as pl
from jax.experimental.pallas import tpu as pltpu
from jax.sharding import PartitionSpec as P


C = 128
TRI_DIM = 16
HEAD_DIM = 48
LANES = 128

epsilon = 1e-05
cap_value = 10.0
rel_reach = 32.0

F32 = jnp.float32
BF16 = jnp.bfloat16
VMEM = pl.BlockSpec(memory_space=pltpu.VMEM)
SMEM = pl.BlockSpec(memory_space=pltpu.SMEM)
ANY = pl.BlockSpec(memory_space=pl.ANY)


def on_chip(x):
    return pltpu.with_memory_space_constraint(x, pltpu.VMEM)


def call(kernel, out_shape, smem, near=(), far=(), scratch=()):
    many = isinstance(out_shape, (tuple, list))
    return pl.pallas_call(
        kernel,
        out_shape=out_shape,
        in_specs=[SMEM] * len(smem) + [VMEM] * len(near) + [ANY] * len(far),
        out_specs=tuple([VMEM] * len(out_shape)) if many else VMEM,
        scratch_shapes=list(scratch),
    )(*smem, *[on_chip(x) for x in near], *far)


def chip(x):
    return pltpu.VMEM(x.shape, x.dtype)


def mm(a, b):
    return jnp.dot(a, b, preferred_element_type=F32)


def mm_nt(a, b):
    return lax.dot_general(a, b, (((1,), (1,)), ((), ())), preferred_element_type=F32)


def mm_tn(a, b):
    return lax.dot_general(a, b, (((0,), (0,)), ((), ())), preferred_element_type=F32)


def iota(shape, dim):
    return lax.broadcasted_iota(jnp.int32, shape, dim)


def layer_norm(x, gain):
    centered = x - jnp.mean(x, -1, keepdims=True)
    spread = jnp.mean(centered * centered, -1, keepdims=True)
    return centered * lax.rsqrt(spread + epsilon) * gain


def feature(x):
    return jnp.where(x > 0, x + 1.0, jnp.exp(x))


def sigmoid(x):
    return 0.5 * jnp.tanh(0.5 * x) + 0.5


GROUP = 4


def triangle_lines(lines, valid, same_head, gain, qk, vg, out, scale):
    tokens = lines[0].shape[0]
    x = jnp.concatenate(lines, axis=0)
    normed = layer_norm(x, gain).astype(BF16)
    query_key, value_gate = mm(normed, qk), mm(normed, vg)
    each = [slice(n * tokens, (n + 1) * tokens) for n in range(len(lines))]
    keys = [jnp.where(valid, feature(query_key[rows, C:]), 0.0).astype(BF16) for rows in each]
    values = value_gate[:, :C].astype(BF16)
    states = [
        jnp.where(same_head, mm_tn(key, values[rows]) * scale, 0.0).astype(BF16) for key, rows in zip(keys, each)
    ]
    queries = feature(query_key[:, :C]).astype(BF16)
    gate = sigmoid(value_gate[:, C:])
    mixed = jnp.concatenate([mm(queries[rows], state) for state, rows in zip(states, each)], axis=0)
    x = x + mm((gate * mixed).astype(BF16), out)
    return [x[rows] for rows in each]


def masks(tokens, mask_ref):
    valid = iota((tokens, C), 0) < jnp.sum(mask_ref[...])
    same_head = (iota((C, C), 0) // TRI_DIM) == (iota((C, C), 1) // TRI_DIM)
    return valid, same_head


def row_kernel(scale, n_col, lines, mask_ref, gain_ref, qk_ref, vg_ref, out_w_ref, own_ref, *refs):
    pieces, z_ref, x_scr, z_scr = refs[:-3], refs[-3], refs[-2], refs[-1]
    block = own_ref.shape[0] // lines
    tokens = block * n_col
    me = lax.axis_index("col")
    for k in range(n_col):
        source = me ^ k
        for line in range(lines):
            start = pl.multiple_of(line * tokens + source * block, block)
            rows = slice(line * block, (line + 1) * block)
            piece = pieces[k - 1][rows, :] if k else own_ref[rows, :]
            x_scr[pl.ds(start, block), :] = piece.astype(F32)
    valid, same_head = masks(tokens, mask_ref)
    owners, per_owner, _ = z_ref.shape
    per_line = per_owner // lines
    for first in range(0, lines, GROUP):
        group = [x_scr[line * tokens : (line + 1) * tokens, :] for line in range(first, first + GROUP)]
        group = triangle_lines(group, valid, same_head, gain_ref[0:1, :], qk_ref[0], vg_ref[0], out_w_ref[0], scale)
        for n, z in enumerate(group):
            for m in range(per_line):
                for o in range(owners // 8):
                    base = 8 * (o * per_owner + (first + n) * per_line + m)
                    z_scr[base : base + 8, :] = z[m * owners + o * 8 :][:8]
    for d in range(owners):
        z_ref[d] = z_scr[pl.ds(d // 8 * 8 * per_owner + d % 8, per_owner, stride=8), :].astype(BF16)


def bias_form(row_count, lines, heads_here):
    side = LANES // (row_count * lines)
    return side, heads_here // side


def col_kernel(
    scale, n_row, n_col, row_count, col_count, heads_here,
    mask_ref, gain_ref, qk_ref, vg_ref, out_w_ref, bias_gain_ref, bias_proj_ref, z_ref, out_ref, z_scr, out_scr,
):
    lines = z_scr.shape[0] // (n_row * row_count)
    tokens = n_row * row_count
    devices = n_row * n_col
    z_scr[...] = z_ref[...].astype(F32)
    valid, same_head = masks(tokens, mask_ref)
    done, normed = [], []
    for first in range(0, lines, GROUP):
        group = [z_scr[pl.ds(line, tokens, stride=lines), :] for line in range(first, first + GROUP)]
        group = triangle_lines(group, valid, same_head, gain_ref[1:2, :], qk_ref[1], vg_ref[1], out_w_ref[1], scale)
        for x in group:
            done.append(x.astype(BF16).astype(F32))
            normed.append(layer_norm(done[-1], bias_gain_ref[...]).astype(BF16))
    side, deep = bias_form(row_count, lines, heads_here)
    chunk = row_count + deep
    proj = bias_proj_ref[...].astype(F32)
    projs = []
    for g in range(side):
        first = [c * heads_here + g * deep for c in range(n_col)]
        projs.append(jnp.concatenate([proj[f : f + deep] for f in first], axis=0).astype(BF16))
    for r in range(n_row):
        rows = slice(r * row_count, (r + 1) * row_count)
        here = jnp.concatenate([part[rows] for part in normed], axis=0)
        bias = jnp.concatenate([mm_nt(p, here) for p in projs], axis=1)
        for c in range(n_col):
            base = (r * n_col + c) * chunk
            out_scr[base : base + row_count, :] = done[c * col_count // devices][rows]
            out_scr[base + row_count : base + chunk, :] = bias[c * deep : (c + 1) * deep, :]
    out_ref[...] = out_scr[...].astype(BF16)


def start_all(pairs, sems):
    copies = [pltpu.make_async_copy(a, b, sems.at[n]) for n, (a, b) in enumerate(pairs)]
    for copy in copies:
        copy.start()
    return copies


def wait_all(copies):
    for copy in copies:
        copy.wait()


def kv_kernel(count, single_ref, gain_ref, qk_ref, vg_ref, x_ref, *refs):
    rest, (kv_ref, normed_ref, own_ref), rest_out, (single, gain, wk, wv, sems) = (
        refs[:count], refs[count : count + 3], refs[count + 3 : -5], refs[-5:],
    )
    pairs = [(single_ref, single), (gain_ref, gain), (qk_ref.at[1], wk), (vg_ref.at[0], wv)]
    pairs += [(x_ref.at[lax.axis_index("col")], own_ref), *zip(rest, rest_out)]
    copies = start_all(pairs, sems)
    wait_all(copies[:2])
    gains = jnp.concatenate([gain[c : c + 1, :] for c in range(gain.shape[0])], axis=1)
    normed = layer_norm(single[...].astype(F32), gains).astype(BF16)
    normed_ref[...] = normed
    copies[2].wait()
    kv_ref[0] = mm_nt(normed, wk[...]).astype(BF16)
    copies[3].wait()
    kv_ref[1] = mm_nt(normed, wv[...]).astype(BF16)
    wait_all(copies[4:])


def qg_kernel(normed_ref, qk_ref, vg_ref, q_ref, g_ref):
    q_ref[...] = mm_nt(normed_ref[...], qk_ref[0]).astype(BF16)
    g_ref[...] = mm_nt(normed_ref[...], vg_ref[1])


def attn_kernel(
    n_row, n_col, row_count, heads_here,
    slots, chain_bias_ref, slope_ref, mask_ref, chain_ref, residue_ref, q_ref, g_ref, out_w_ref, got_ref, *refs,
):
    kv_refs, o_refs, (k_scr, v_scr, o_scr, got_scr) = refs[: -4 - n_col], refs[-4 - n_col : -4], refs[-4:]
    tokens = n_row * row_count
    devices = n_row * n_col
    lines = tokens // devices
    width = heads_here * HEAD_DIM
    me = lax.axis_index("row")
    held = [(ref, t) for ref in kv_refs for t in range(ref.shape[0])]
    for slot, (ref, t) in zip(slots, held):
        start = pl.multiple_of((me ^ slot) * row_count, row_count)
        k_scr[pl.ds(start, row_count), :] = ref[t, 0].astype(F32)
        v_scr[pl.ds(start, row_count), :] = ref[t, 1].astype(F32)
    keys, values = k_scr[...].astype(BF16), v_scr[...].astype(BF16)

    own = iota((row_count, tokens), 1) == iota((row_count, tokens), 0) + me * row_count
    chain = chain_ref[...].astype(F32)
    residue = residue_ref[...].astype(F32)
    my_chain = jnp.sum(jnp.where(own, chain, 0.0), -1, keepdims=True)
    my_residue = jnp.sum(jnp.where(own, residue, 0.0), -1, keepdims=True)
    same_chain = my_chain == chain
    offset = jnp.clip(my_residue - residue, -rel_reach, rel_reach) / rel_reach
    length = jnp.sum(mask_ref[...])
    valid = iota((row_count, tokens), 1) < length

    _, deep = bias_form(row_count, lines, heads_here)
    chunk = row_count + deep
    got_scr[...] = got_ref[...].astype(F32)
    same = (iota((devices, devices), 0) == iota((devices, devices), 1)).astype(F32).astype(BF16)
    turned = [
        mm_tn(got_scr[pl.ds(row_count + a, devices, stride=chunk), :].astype(BF16), same) for a in range(deep)
    ]

    head_of = iota((row_count, width), 1) // HEAD_DIM
    query = q_ref[...].astype(F32)
    stacked = jnp.concatenate(
        [jnp.where(head_of == h, query, 0.0) for h in range(heads_here)], axis=0
    ).astype(BF16)
    scores = mm_nt(stacked, keys) / math.sqrt(HEAD_DIM)
    weights = []
    for h in range(heads_here):
        bias = jnp.concatenate(
            [
                turned[h % deep][(h // deep * lines + line) * row_count :][:row_count]
                for line in range(lines)
            ],
            axis=1,
        )
        e = scores[h * row_count : (h + 1) * row_count] + bias
        e = e + jnp.where(same_chain, chain_bias_ref[0:1, h : h + 1] + slope_ref[0:1, h : h + 1] * offset, 0.0)
        weights.append(jnp.where(valid, jnp.exp(cap_value * jnp.tanh(e / cap_value)), 0.0))
    numerator = mm(jnp.concatenate(weights, axis=0).astype(BF16), values)
    attended = jnp.zeros((row_count, width), F32)
    for h in range(heads_here):
        part = numerator[h * row_count : (h + 1) * row_count] / jnp.sum(weights[h], -1, keepdims=True)
        attended = jnp.where(head_of == h, part, attended)
    gated = (sigmoid(g_ref[...]) * attended).astype(BF16)
    full = mm(gated, out_w_ref[...])
    share = full.shape[1] // n_col
    for c in range(n_col):
        o_scr[c] = full[:, c * share : (c + 1) * share]
    for k in range(n_col):
        o_refs[k][...] = o_scr[lax.axis_index("col") ^ k].astype(BF16)


def pair_kernel(row_count, chunk, got_ref, out_ref, scr):
    scr[...] = got_ref[...].astype(F32)
    for i in range(row_count):
        out_ref[i] = scr[pl.ds(i, out_ref.shape[1], stride=chunk), :].astype(BF16)


def pick_kernel(n_col, x_ref, *refs):
    me = lax.axis_index("col")
    wait_all(start_all([(x_ref.at[me ^ (k + 1)], refs[k]) for k in range(n_col - 1)], refs[-1]))


def swap_col(blocks, n_col):
    got = []
    for k, block in enumerate(blocks, 1):
        got.append(lax.ppermute(block, "col", [(i, i ^ k) for i in range(n_col)]))
    return got


def in_layer(n_row, n_col, *args):
    return on_device(n_row, n_col, *args)


def on_device(
    n_row, n_col,
    pair_act, single, token_mask, chain_index, residue_index, tri_gain, tri_qk, tri_vg, tri_out,
    bias_gain, bias_proj, chain_bias, pos_slope, attn_gain, attn_qk, attn_vg, attn_out,
):
    tokens = token_mask.shape[0]
    row_count, col_count = pair_act.shape[0], pair_act.shape[1]
    heads_here = chain_bias.shape[0]
    devices = n_row * n_col
    own_rows, own_cols = row_count // n_col, tokens // devices
    scale = 1.0 / (2.0 * TRI_DIM * math.sqrt(tokens))
    width = heads_here * HEAD_DIM
    share = attn_out.shape[1] // n_col
    chunk = row_count + bias_form(row_count, own_cols, heads_here)[1]

    blocks = pair_act.reshape(n_col, own_rows * col_count, C)
    block = pltpu.VMEM(blocks.shape[1:], BF16)
    picked = call(
        functools.partial(pick_kernel, n_col), [block] * (n_col - 1),
        [], [], [blocks], [pltpu.SemaphoreType.DMA((n_col - 1,))],
    )
    pieces = swap_col(picked, n_col)
    wqk, wvg = attn_qk.swapaxes(1, 2), attn_vg.swapaxes(1, 2)
    weight = pltpu.VMEM(wqk.shape[1:], BF16)
    gain2 = attn_gain.reshape(-1, C)
    rest = [
        token_mask.reshape(1, tokens), tri_gain, tri_qk, tri_vg, tri_out, bias_gain.reshape(1, C), bias_proj.T,
        chain_bias.reshape(1, -1), pos_slope.reshape(1, -1), chain_index.reshape(1, tokens),
        residue_index.reshape(1, tokens),
    ]
    kv, normed, own, *rest = call(
        functools.partial(kv_kernel, len(rest)),
        [pltpu.VMEM((2, row_count, width), BF16), chip(single), block, *map(chip, rest)],
        [], [], [single, gain2, wqk, wvg, blocks, *rest],
        [chip(single), chip(gain2), weight, weight, pltpu.SemaphoreType.DMA((5 + len(rest),))],
    )
    mask, tri_gain, tri_qk, tri_vg, tri_out, bias_gain, bias_proj, chain_bias, pos_slope, chain, residue = rest
    z_out = call(
        functools.partial(row_kernel, scale, n_col, own_rows),
        pltpu.VMEM((devices, own_rows * own_cols, C), BF16),
        [], [mask, tri_gain, tri_qk, tri_vg, tri_out, own, *pieces],
        scratch=[pltpu.VMEM((own_rows * tokens, C), F32)] * 2,
    )

    z_in = lax.all_to_all(z_out, ("row", "col"), 0, 0, tiled=True)
    query, gate = call(
        qg_kernel, [pltpu.VMEM((row_count, width), BF16), pltpu.VMEM((row_count, width), F32)],
        [], [normed, wqk, wvg],
    )
    back = call(
        functools.partial(col_kernel, scale, n_row, n_col, row_count, col_count, heads_here),
        pltpu.VMEM((devices * chunk, C), BF16),
        [],
        [
            mask, tri_gain, tri_qk, tri_vg, tri_out, bias_gain, bias_proj,
            z_in.reshape(own_cols * tokens, C),
        ],
        scratch=[pltpu.VMEM((own_cols * tokens, C), F32), pltpu.VMEM((devices * chunk, C), F32)],
    )
    def kv_from(sent, step):
        return lax.ppermute(sent, "row", [(i, i ^ step) for i in range(n_row)])

    held, slots = [kv[None]], [0]
    if n_row > 1:
        held.append(kv_from(held[0], 1))
        slots.append(1)
    if n_row > 2:
        both = jnp.concatenate(held, axis=0)
        for step in range(2, n_row, 2):
            held.append(kv_from(both, step))
            slots += [step, step ^ 1]
    back, held = lax.optimization_barrier((back, held))
    got = lax.all_to_all(back.reshape(devices, chunk // 2, 2, C), ("row", "col"), 0, 0, tiled=True)
    got = got.reshape(devices * chunk, C)

    terms = call(
        functools.partial(attn_kernel, n_row, n_col, row_count, heads_here, slots),
        [pltpu.VMEM((row_count, share), BF16)] * n_col,
        [],
        [chain_bias, pos_slope, mask, chain, residue, query, gate, attn_out, got, *held],
        scratch=[pltpu.VMEM((tokens, width), F32)] * 2
        + [pltpu.VMEM((n_col, row_count, share), F32), pltpu.VMEM((devices * chunk, C), F32)],
    )
    parts = [terms[0]] + swap_col(terms[1:], n_col)
    token_update = sum(part.astype(F32) for part in parts).astype(BF16)

    first = lax.axis_index("col") * col_count % devices
    mine = got if col_count == devices else lax.dynamic_slice_in_dim(got, first * chunk, col_count * chunk, 0)
    pair_out = call(
        functools.partial(pair_kernel, row_count, chunk),
        jax.ShapeDtypeStruct((row_count, col_count, C), BF16),
        [], [mine], scratch=[pltpu.VMEM((col_count * chunk, C), F32)],
    )
    return (pair_out, token_update)


def solution(mesh):
    return jax.shard_map(
        functools.partial(in_layer, mesh.shape["row"], mesh.shape["col"]),
        mesh=mesh,
        in_specs=(
            P(("grp", "row"), "col", None),
            P(("grp", "row"), None),
            P("grp"),
            P("grp"),
            P("grp"),
            P(),
            P(),
            P(),
            P(),
            P(),
            P(),
            P("col"),
            P("col"),
            P(),
            P(None, None, "col"),
            P(None, None, "col"),
            P("col", None),
        ),
        out_specs=(P(("grp", "row"), "col", None), P(("grp", "row"), "col")),
        check_vma=False,
    )
```

```python
import functools
import math

import jax
import jax.numpy as jnp
from jax import lax
from jax.experimental import pallas as pl
from jax.experimental.pallas import tpu as pltpu
from jax.sharding import PartitionSpec as P


C = 128
TRI_DIM = 16
HEAD_DIM = 48
LANES = 128

epsilon = 1e-05
cap_value = 10.0
rel_reach = 32.0

F32 = jnp.float32
BF16 = jnp.bfloat16
VMEM = pl.BlockSpec(memory_space=pltpu.VMEM)
SMEM = pl.BlockSpec(memory_space=pltpu.SMEM)
ANY = pl.BlockSpec(memory_space=pl.ANY)


def on_chip(x):
    return pltpu.with_memory_space_constraint(x, pltpu.VMEM)


def call(kernel, out_shape, smem, near=(), far=(), scratch=()):
    many = isinstance(out_shape, (tuple, list))
    return pl.pallas_call(
        kernel,
        out_shape=out_shape,
        in_specs=[SMEM] * len(smem) + [VMEM] * len(near) + [ANY] * len(far),
        out_specs=tuple([VMEM] * len(out_shape)) if many else VMEM,
        scratch_shapes=list(scratch),
    )(*smem, *[on_chip(x) for x in near], *far)


def chip(x):
    return pltpu.VMEM(x.shape, x.dtype)


def mm(a, b):
    return jnp.dot(a, b, preferred_element_type=F32)


def mm_nt(a, b):
    return lax.dot_general(a, b, (((1,), (1,)), ((), ())), preferred_element_type=F32)


def mm_tn(a, b):
    return lax.dot_general(a, b, (((0,), (0,)), ((), ())), preferred_element_type=F32)


def iota(shape, dim):
    return lax.broadcasted_iota(jnp.int32, shape, dim)


def layer_norm(x, gain):
    centered = x - jnp.mean(x, -1, keepdims=True)
    spread = jnp.mean(centered * centered, -1, keepdims=True)
    return centered * lax.rsqrt(spread + epsilon) * gain


def feature(x):
    return jnp.where(x > 0, x + 1.0, jnp.exp(x))


def sigmoid(x):
    return jax.nn.sigmoid(x)


GROUP = 4


def triangle_lines(lines, valid, same_head, gain, qk, vg, out, scale):
    tokens = lines[0].shape[0]
    x = jnp.concatenate(lines, axis=0)
    normed = layer_norm(x, gain).astype(BF16)
    query_key, value_gate = mm(normed, qk), mm(normed, vg)
    each = [slice(n * tokens, (n + 1) * tokens) for n in range(len(lines))]
    keys = [feature(query_key[rows, C:]).astype(BF16) for rows in each]
    values = jnp.concatenate([jnp.where(valid, value_gate[rows, :C], 0.0).astype(BF16) for rows in each], axis=0)
    states = [
        jnp.where(same_head, mm_tn(key, values[rows]) * scale, 0.0).astype(BF16) for key, rows in zip(keys, each)
    ]
    queries = [feature(query_key[rows, :C]).astype(BF16) for rows in each]
    gates = [sigmoid(value_gate[rows, C:]) for rows in each]
    mixed = [mm(query, state) for query, state in zip(queries, states)]
    return [line + mm((gate * mix).astype(BF16), out) for line, gate, mix in zip(lines, gates, mixed)]


def masks(tokens, mask_ref):
    valid = iota((tokens, C), 0) < jnp.sum(mask_ref[...])
    same_head = (iota((C, C), 0) // TRI_DIM) == (iota((C, C), 1) // TRI_DIM)
    return valid, same_head


def row_kernel(scale, n_col, lines, mask_ref, gain_ref, qk_ref, vg_ref, out_w_ref, own_ref, *refs):
    pieces, z_ref, x_scr, z_scr = refs[:-3], refs[-3], refs[-2], refs[-1]
    block = own_ref.shape[0] // lines
    tokens = block * n_col
    me = lax.axis_index("col")
    for k in range(n_col):
        source = me ^ k
        for line in range(lines):
            start = pl.multiple_of(line * tokens + source * block, block)
            rows = slice(line * block, (line + 1) * block)
            piece = pieces[k - 1][rows, :] if k else own_ref[rows, :]
            x_scr[pl.ds(start, block), :] = piece.astype(F32)
    valid, same_head = masks(tokens, mask_ref)
    owners, per_owner, _ = z_ref.shape
    per_line = per_owner // lines
    for first in range(0, lines, GROUP):
        group = [x_scr[line * tokens : (line + 1) * tokens, :] for line in range(first, first + GROUP)]
        group = triangle_lines(group, valid, same_head, gain_ref[0:1, :], qk_ref[0], vg_ref[0], out_w_ref[0], scale)
        for n, z in enumerate(group):
            for m in range(per_line):
                for o in range(owners // 8):
                    base = 8 * (o * per_owner + (first + n) * per_line + m)
                    z_scr[base : base + 8, :] = z[m * owners + o * 8 :][:8]
    for d in range(owners):
        z_ref[d] = z_scr[pl.ds(d // 8 * 8 * per_owner + d % 8, per_owner, stride=8), :].astype(BF16)


def bias_form(row_count, lines, heads_here):
    side = LANES // (row_count * lines)
    return side, heads_here // side


def col_kernel(
    scale, n_row, n_col, row_count, col_count, heads_here,
    mask_ref, gain_ref, qk_ref, vg_ref, out_w_ref, bias_gain_ref, bias_proj_ref, z_ref, out_ref, z_scr, out_scr,
):
    lines = z_scr.shape[0] // (n_row * row_count)
    tokens = n_row * row_count
    devices = n_row * n_col
    z_scr[...] = z_ref[...].astype(F32)
    valid, same_head = masks(tokens, mask_ref)
    done, normed = [], []
    for first in range(0, lines, GROUP):
        group = [z_scr[pl.ds(line, tokens, stride=lines), :] for line in range(first, first + GROUP)]
        group = triangle_lines(group, valid, same_head, gain_ref[1:2, :], qk_ref[1], vg_ref[1], out_w_ref[1], scale)
        for x in group:
            done.append(x.astype(BF16).astype(F32))
            normed.append(layer_norm(done[-1], bias_gain_ref[...]).astype(BF16))
    side, deep = bias_form(row_count, lines, heads_here)
    chunk = row_count + deep
    proj = bias_proj_ref[...].astype(F32)
    projs = []
    for g in range(side):
        first = [c * heads_here + g * deep for c in range(n_col)]
        projs.append(jnp.concatenate([proj[f : f + deep] for f in first], axis=0).astype(BF16))
    for r in range(n_row):
        rows = slice(r * row_count, (r + 1) * row_count)
        here = jnp.concatenate([part[rows] for part in normed], axis=0)
        bias = jnp.concatenate([mm_nt(p, here) for p in projs], axis=1)
        for c in range(n_col):
            base = (r * n_col + c) * chunk
            out_scr[base : base + row_count, :] = done[c * col_count // devices][rows]
            out_scr[base + row_count : base + chunk, :] = bias[c * deep : (c + 1) * deep, :]
    out_ref[...] = out_scr[...].astype(BF16)


def start_all(pairs, sems):
    copies = [pltpu.make_async_copy(a, b, sems.at[n]) for n, (a, b) in enumerate(pairs)]
    for copy in copies:
        copy.start()
    return copies


def wait_all(copies):
    for copy in copies:
        copy.wait()


def kv_kernel(count, single_ref, gain_ref, qk_ref, vg_ref, x_ref, *refs):
    rest, (kv_ref, normed_ref, own_ref), rest_out, (single, gain, wk, wv, sems) = (
        refs[:count], refs[count : count + 3], refs[count + 3 : -5], refs[-5:],
    )
    pairs = [(single_ref, single), (gain_ref, gain), (qk_ref.at[1], wk), (vg_ref.at[0], wv)]
    pairs += [(x_ref.at[lax.axis_index("col")], own_ref), *zip(rest, rest_out)]
    copies = start_all(pairs, sems)
    wait_all(copies[:2])
    gains = jnp.concatenate([gain[c : c + 1, :] for c in range(gain.shape[0])], axis=1)
    normed = layer_norm(single[...].astype(F32), gains).astype(BF16)
    normed_ref[...] = normed
    copies[2].wait()
    kv_ref[0] = mm_nt(normed, wk[...]).astype(BF16)
    copies[3].wait()
    kv_ref[1] = mm_nt(normed, wv[...]).astype(BF16)
    wait_all(copies[4:])


def qg_kernel(normed_ref, qk_ref, vg_ref, q_ref, g_ref):
    q_ref[...] = mm_nt(normed_ref[...], qk_ref[0]).astype(BF16)
    g_ref[...] = mm_nt(normed_ref[...], vg_ref[1])


def attn_kernel(
    n_row, n_col, row_count, heads_here,
    slots, chain_bias_ref, slope_ref, mask_ref, chain_ref, residue_ref, q_ref, g_ref, out_w_ref, got_ref, *refs,
):
    kv_refs, o_refs, (k_scr, v_scr, o_scr, got_scr) = refs[: -4 - n_col], refs[-4 - n_col : -4], refs[-4:]
    tokens = n_row * row_count
    devices = n_row * n_col
    lines = tokens // devices
    width = heads_here * HEAD_DIM
    me = lax.axis_index("row")
    held = [(ref, t) for ref in kv_refs for t in range(ref.shape[0])]
    for slot, (ref, t) in zip(slots, held):
        start = pl.multiple_of((me ^ slot) * row_count, row_count)
        k_scr[pl.ds(start, row_count), :] = ref[t, 0].astype(F32)
        v_scr[pl.ds(start, row_count), :] = ref[t, 1].astype(F32)
    keys, values = k_scr[...].astype(BF16), v_scr[...].astype(BF16)

    own = iota((row_count, tokens), 1) == iota((row_count, tokens), 0) + me * row_count
    chain = chain_ref[...].astype(F32)
    residue = residue_ref[...].astype(F32)
    my_chain = jnp.sum(jnp.where(own, chain, 0.0), -1, keepdims=True)
    my_residue = jnp.sum(jnp.where(own, residue, 0.0), -1, keepdims=True)
    same_chain = my_chain == chain
    offset = jnp.clip(my_residue - residue, -rel_reach, rel_reach) / rel_reach
    length = jnp.sum(mask_ref[...])
    valid = iota((row_count, tokens), 1) < length

    _, deep = bias_form(row_count, lines, heads_here)
    chunk = row_count + deep
    got_scr[...] = got_ref[...].astype(F32)
    same = (iota((devices, devices), 0) == iota((devices, devices), 1)).astype(F32).astype(BF16)
    turned = [
        mm_tn(got_scr[pl.ds(row_count + a, devices, stride=chunk), :].astype(BF16), same) for a in range(deep)
    ]

    head_of = iota((row_count, width), 1) // HEAD_DIM
    query = q_ref[...].astype(F32)
    stacked = jnp.concatenate(
        [jnp.where(head_of == h, query, 0.0) for h in range(heads_here)], axis=0
    ).astype(BF16)
    scores = mm_nt(stacked, keys) / math.sqrt(HEAD_DIM)
    weights = []
    for h in range(heads_here):
        bias = jnp.concatenate(
            [
                turned[h % deep][(h // deep * lines + line) * row_count :][:row_count]
                for line in range(lines)
            ],
            axis=1,
        )
        e = scores[h * row_count : (h + 1) * row_count] + bias
        e = e + jnp.where(same_chain, chain_bias_ref[0:1, h : h + 1] + slope_ref[0:1, h : h + 1] * offset, 0.0)
        weights.append(jnp.where(valid, jnp.exp(cap_value * jnp.tanh(e / cap_value)), 0.0))
    numerator = mm(jnp.concatenate(weights, axis=0).astype(BF16), values)
    attended = jnp.zeros((row_count, width), F32)
    for h in range(heads_here):
        part = numerator[h * row_count : (h + 1) * row_count] / jnp.sum(weights[h], -1, keepdims=True)
        attended = jnp.where(head_of == h, part, attended)
    gated = (sigmoid(g_ref[...]) * attended).astype(BF16)
    full = mm(gated, out_w_ref[...])
    share = full.shape[1] // n_col
    for c in range(n_col):
        o_scr[c] = full[:, c * share : (c + 1) * share]
    for k in range(n_col):
        o_refs[k][...] = o_scr[lax.axis_index("col") ^ k].astype(BF16)


def pair_kernel(row_count, chunk, got_ref, out_ref, scr):
    scr[...] = got_ref[...].astype(F32)
    for i in range(row_count):
        out_ref[i] = scr[pl.ds(i, out_ref.shape[1], stride=chunk), :].astype(BF16)


def pick_kernel(n_col, x_ref, *refs):
    me = lax.axis_index("col")
    wait_all(start_all([(x_ref.at[me ^ (k + 1)], refs[k]) for k in range(n_col - 1)], refs[-1]))


def swap_col(blocks, n_col):
    got = []
    for k, block in enumerate(blocks, 1):
        got.append(lax.ppermute(block, "col", [(i, i ^ k) for i in range(n_col)]))
    return got


def in_layer(n_row, n_col, *args):
    return on_device(n_row, n_col, *args)


def on_device(
    n_row, n_col,
    pair_act, single, token_mask, chain_index, residue_index, tri_gain, tri_qk, tri_vg, tri_out,
    bias_gain, bias_proj, chain_bias, pos_slope, attn_gain, attn_qk, attn_vg, attn_out,
):
    tokens = token_mask.shape[0]
    row_count, col_count = pair_act.shape[0], pair_act.shape[1]
    heads_here = chain_bias.shape[0]
    devices = n_row * n_col
    own_rows, own_cols = row_count // n_col, tokens // devices
    scale = 1.0 / (2.0 * TRI_DIM * math.sqrt(tokens))
    width = heads_here * HEAD_DIM
    share = attn_out.shape[1] // n_col
    chunk = row_count + bias_form(row_count, own_cols, heads_here)[1]

    blocks = pair_act.reshape(n_col, own_rows * col_count, C)
    block = pltpu.VMEM(blocks.shape[1:], BF16)
    picked = call(
        functools.partial(pick_kernel, n_col), [block] * (n_col - 1),
        [], [], [blocks], [pltpu.SemaphoreType.DMA((n_col - 1,))],
    )
    pieces = swap_col(picked, n_col)
    wqk, wvg = attn_qk.swapaxes(1, 2), attn_vg.swapaxes(1, 2)
    weight = pltpu.VMEM(wqk.shape[1:], BF16)
    gain2 = attn_gain.reshape(-1, C)
    rest = [
        token_mask.reshape(1, tokens), tri_gain, tri_qk, tri_vg, tri_out, bias_gain.reshape(1, C), bias_proj.T,
        chain_bias.reshape(1, -1), pos_slope.reshape(1, -1), chain_index.reshape(1, tokens),
        residue_index.reshape(1, tokens),
    ]
    kv, normed, own, *rest = call(
        functools.partial(kv_kernel, len(rest)),
        [pltpu.VMEM((2, row_count, width), BF16), chip(single), block, *map(chip, rest)],
        [], [], [single, gain2, wqk, wvg, blocks, *rest],
        [chip(single), chip(gain2), weight, weight, pltpu.SemaphoreType.DMA((5 + len(rest),))],
    )
    mask, tri_gain, tri_qk, tri_vg, tri_out, bias_gain, bias_proj, chain_bias, pos_slope, chain, residue = rest
    z_out = call(
        functools.partial(row_kernel, scale, n_col, own_rows),
        pltpu.VMEM((devices, own_rows * own_cols, C), BF16),
        [], [mask, tri_gain, tri_qk, tri_vg, tri_out, own, *pieces],
        scratch=[pltpu.VMEM((own_rows * tokens, C), F32)] * 2,
    )

    z_in = lax.all_to_all(z_out.reshape(devices, -1, 2, C), ("row", "col"), 0, 0, tiled=True)
    query, gate = call(
        qg_kernel, [pltpu.VMEM((row_count, width), BF16), pltpu.VMEM((row_count, width), F32)],
        [], [normed, wqk, wvg],
    )
    back = call(
        functools.partial(col_kernel, scale, n_row, n_col, row_count, col_count, heads_here),
        pltpu.VMEM((devices * chunk, C), BF16),
        [],
        [
            mask, tri_gain, tri_qk, tri_vg, tri_out, bias_gain, bias_proj,
            z_in.reshape(own_cols * tokens, C),
        ],
        scratch=[pltpu.VMEM((own_cols * tokens, C), F32), pltpu.VMEM((devices * chunk, C), F32)],
    )
    def kv_from(sent, step):
        return lax.ppermute(sent, "row", [(i, i ^ step) for i in range(n_row)])

    held, slots = [kv[None]], [0]
    if n_row > 1:
        held.append(kv_from(held[0], 1))
        slots.append(1)
    if n_row > 2:
        both = jnp.concatenate(held, axis=0)
        for step in range(2, n_row, 2):
            held.append(kv_from(both, step))
            slots += [step, step ^ 1]
    back, held = lax.optimization_barrier((back, held))
    got = lax.all_to_all(back.reshape(devices, chunk // 2, 2, C), ("row", "col"), 0, 0, tiled=True)
    got = got.reshape(devices * chunk, C)

    terms = call(
        functools.partial(attn_kernel, n_row, n_col, row_count, heads_here, slots),
        [pltpu.VMEM((row_count, share), BF16)] * n_col,
        [],
        [chain_bias, pos_slope, mask, chain, residue, query, gate, attn_out, got, *held],
        scratch=[pltpu.VMEM((tokens, width), F32)] * 2
        + [pltpu.VMEM((n_col, row_count, share), F32), pltpu.VMEM((devices * chunk, C), F32)],
    )
    parts = [terms[0]] + swap_col(terms[1:], n_col)
    token_update = sum(part.astype(F32) for part in parts).astype(BF16)

    first = lax.axis_index("col") * col_count % devices
    mine = got if col_count == devices else lax.dynamic_slice_in_dim(got, first * chunk, col_count * chunk, 0)
    pair_out = call(
        functools.partial(pair_kernel, row_count, chunk),
        jax.ShapeDtypeStruct((row_count, col_count, C), BF16),
        [], [mine], scratch=[pltpu.VMEM((col_count * chunk, C), F32)],
    )
    return (pair_out, token_update)


def solution(mesh):
    return jax.shard_map(
        functools.partial(in_layer, mesh.shape["row"], mesh.shape["col"]),
        mesh=mesh,
        in_specs=(
            P(("grp", "row"), "col", None),
            P(("grp", "row"), None),
            P("grp"),
            P("grp"),
            P("grp"),
            P(),
            P(),
            P(),
            P(),
            P(),
            P(),
            P("col"),
            P("col"),
            P(),
            P(None, None, "col"),
            P(None, None, "col"),
            P("col", None),
        ),
        out_specs=(P(("grp", "row"), "col", None), P(("grp", "row"), "col")),
        check_vma=False,
    )
```
